32 devices in a mesh: row: 8 (over y, x, core), col: 4 (over z).
Axes of the slice: x: 2, y: 2, z: 4, core: 2. Of those that a mesh axis runs over, the one named last changes fastest.
Arguments:
- upper_block: float32 [2, 1024, 1024], P(None, 'row', 'col'), may hold values from -0.1875 to 0.1875
- block_inverse: float32 [2, 1024, 128], P(None, 'row'), may hold values from -0.25 to 0.25
- panel_rhs: float32 [2, 32, 1024], P(None, None, 'row'), may hold values from -6 to 6
- upper_trail: float32 [2, 1024, 65536], P(None, 'row', 'col'), may hold values from -0.125 to 0.125
- trail_rhs: float32 [2, 32, 65536], P(None, None, ('col', 'row')), may hold values from -6 to 6
- currents: float32 [2, 1024], P(None, 'row'), may hold values from -4 to 4
- owner: int32 [1024], P('row'), may hold values from 0 to 127
Outputs:
- panel_adjoint: float32 [2, 32, 1024], P(None, None, 'row')
- trail_updated: float32 [2, 32, 65536], P(None, None, ('col', 'row'))
- patch_gradient: float32 [128], P(('row', 'col'))
The draws below stay inside these ranges and needn't reach their ends.
Inputs may be any that keep to these rules, and one draw needn't show every extreme that they name: owner names a surface patch for each panel unknown.
All inputs are finite; a program needn't handle non-finite values.
Results may differ from the reference program's by a relative error of at most 0.0003.
Values sent between devices are 32-bit elements; how exact they have to be, the bound alone decides.
No kernel may reach another device: no remote copies, remote signals or barrier semaphores. Data moves between devices by JAX's collectives and lax.ppermute only.
A program may use at most 64 MiB of HBM per device.

```python
import jax
import jax.numpy as jnp
from jax import lax

PANEL = 1024
NRHS = 32
PB = 128
TRAIL = 65536
PATCHES = 128


def touch_ends(entries, key, smallest, top_value):
    dims = entries.shape
    place = [jax.random.randint(jax.random.fold_in(key, axis), (), 0, dims[axis]) for axis in range(len(dims))]
    entries = entries.at[tuple(place)].set(smallest)
    longest = dims.index(max(dims))
    place[longest] = (place[longest] + 1) % dims[longest]
    return entries.at[tuple(place)].set(top_value)


def shard_levels(own_key, extent, shards, smallest, top_value):
    def one(axis_at, shards_of):
        draws = jax.random.uniform(jax.random.fold_in(jax.random.fold_in(own_key, 6), axis_at), (shards_of,), jnp.float32, smallest / len(shards), top_value / len(shards))
        return jnp.repeat(jnp.exp(draws), extent[axis_at] // shards_of).reshape((-1,) + (1,) * (len(extent) - axis_at - 1))

    level = one(*shards[0])
    for cut in shards[1:]:
        level = level * one(*cut)
    return level


def noise(stream_key, dims, deviation, bound, pieces=(), dtype=jnp.bfloat16):
    entries = jax.random.normal(stream_key, dims, jnp.float32) * deviation
    if len(pieces) > 0:
        entries = shard_levels(stream_key, dims, pieces, -0.22, 0.18) * entries
    return jnp.clip(entries, min=-bound, max=bound).astype(dtype)


def setup_inputs(seed: int = 0) -> dict:
    keys = jax.random.split(jax.random.key(seed), 8)
    return {
        "upper_block": noise(keys[0], (2, PANEL, PANEL), (8 * PB) ** -0.5, 0.1875, ((1, 8), (2, 4)), jnp.float32),
        "block_inverse": noise(keys[1], (2, PANEL, PB), (4 * PB) ** -0.5, 0.25, ((1, 8),), jnp.float32),
        "panel_rhs": noise(keys[2], (2, NRHS, PANEL), 1.0, 6.0, ((2, 8),), jnp.float32),
        "upper_trail": noise(keys[3], (2, PANEL, TRAIL), (2 * PANEL) ** -0.5, 0.125, ((1, 8), (2, 4)), jnp.float32),
        "trail_rhs": noise(keys[4], (2, NRHS, TRAIL), 1.0, 6.0, ((2, 32),), jnp.float32),
        "currents": noise(keys[5], (2, PANEL), 0.3, 4.0, ((1, 8),), jnp.float32),
        "owner": touch_ends(jax.random.randint(keys[6], (PANEL,), 0, PATCHES), jax.random.fold_in(keys[6], 1), 0, PATCHES - 1).astype(jnp.int32),
    }


highest = lax.Precision.HIGHEST


def product_high(first, second):
    return jnp.dot(first, second, precision=highest, preferred_element_type=jnp.float32)


def conj_product(left, right):
    real_part = product_high(left[0], right[0]) + product_high(left[1], right[1])
    imag_part = product_high(left[1], right[0]) - product_high(left[0], right[1])
    return jnp.stack([real_part, imag_part])


def sweep(upper, inverses, rhs, width):
    count = rhs.shape[2] // width
    held_start = jnp.zeros(rhs.shape, jnp.float32)
    solved_start = jnp.zeros(rhs.shape, jnp.float32)

    def advance(index, carry):
        held, solved = carry
        start = (jnp.asarray(index) * width).astype(jnp.int32)
        local = lax.dynamic_slice_in_dim(held, start, width, 2)
        residual = lax.dynamic_slice_in_dim(rhs, start, width, 2) - local
        inverse = lax.dynamic_slice_in_dim(inverses, start, width, 1)
        value = conj_product(residual, inverse)
        rows_here = lax.dynamic_slice_in_dim(upper, start, width, 1)
        held = held + conj_product(value, rows_here)
        solved = lax.dynamic_update_slice_in_dim(solved, value, start, 2)
        return held, solved

    return lax.fori_loop(0, count, advance, (held_start, solved_start))[1]


def reference(upper_block, block_inverse, panel_rhs, upper_trail, trail_rhs, currents, owner):
    solved = sweep(upper_block, block_inverse, panel_rhs, PB)
    updated = trail_rhs - conj_product(solved, upper_trail)
    total = jnp.sum(solved, axis=1)
    partial_value = currents[0] * total[0] - currents[1] * total[1]
    gradient = jax.ops.segment_sum(partial_value, owner, num_segments=PATCHES)
    return solved, updated, gradient
```

```python
import functools

import jax
import jax.numpy as jnp
from jax import lax
from jax.experimental import pallas as pl
from jax.experimental.pallas import tpu as pltpu
from jax.sharding import PartitionSpec as P

PATCH_DEV = 4
LANES = 128
CHUNKS = 2

highest = lax.Precision.HIGHEST


def dot32(first, second):
    return jnp.dot(first, second, precision=highest, preferred_element_type=jnp.float32)


def dot16(first, second):
    return jnp.dot(first, second, preferred_element_type=jnp.float32)


def split(x):
    high = x.astype(jnp.bfloat16)
    return high, (x - high.astype(jnp.float32)).astype(jnp.bfloat16)


def product(left, right):
    rows, depth = left.shape[1], left.shape[2]
    first = jnp.concatenate([left[0], left[1]], axis=0)
    second = jnp.concatenate([left[1], -left[0]], axis=0)
    if depth % LANES == 0:
        joined = jnp.concatenate([first, second], axis=1)
        return dot32(joined, right.reshape(2 * depth, right.shape[2]))
    return dot32(first, right[0]) + dot32(second, right[1])


def step_kernel(step, members, width, *refs):
    refs = list(refs)
    out = refs.pop()
    rhs = [refs.pop(0) for _ in range(members)]
    inverse = [refs.pop(0) for _ in range(members)]
    inside = [refs.pop(0) for _ in range(members - 1)]
    earlier = refs.pop(0) if step else None
    pieces = refs
    observers = rhs[0].shape[1]
    held = None
    for group in range(step):
        for t in range(members):
            x = earlier[2 * group : 2 * group + 2, :, t * width : (t + 1) * width]
            term = product(x, pieces[(step - group - 1) * members + t][...])
            held = term if held is None else held + term
    solved = []
    for b in range(members):
        residual = jnp.concatenate([rhs[b][0], rhs[b][1]], axis=0)
        if held is not None:
            residual = residual - held[:, b * width : (b + 1) * width]
        for a in range(b):
            residual = residual - product(solved[a], inside[a][:, :, b * width : (b + 1) * width])
        value = product(residual.reshape(2, observers, width), inverse[b][...])
        solved.append(value.reshape(2, observers, width))
    if step:
        out[0 : 2 * step] = earlier[...]
    for b in range(members):
        out[2 * step : 2 * step + 2, :, b * width : (b + 1) * width] = solved[b]


def whole(shape):
    return jax.ShapeDtypeStruct(shape, jnp.float32)


def halve(values, axis, bit, rows):
    low = lax.index_in_dim(values, 0, axis, keepdims=False)
    high = lax.index_in_dim(values, 1, axis, keepdims=False)
    arrived = lax.ppermute(high, "row", [(i, i ^ (1 << bit)) for i in range(rows)])
    return low + arrived


def trail_kernel(members, devices, cols, flags, x_in, x_own, currents, owner, trail, sent, kept):
    row, col, last = flags[0], flags[1], flags[2]
    index = pl.program_id(0)
    half = devices // 2
    x = jnp.where(last == 1, x_own[...], x_in[...])
    observers, depth = x.shape[1], x.shape[2]
    first = jnp.concatenate([x[0], x[1]], axis=0)
    second = jnp.concatenate([x[1], -x[0]], axis=0)
    n = trail.shape[2]
    if depth % LANES == 0:
        high, low = split(jnp.concatenate([first, second], axis=1))
        pairs = [(high, low, trail[...].reshape(2 * depth, n))]
    else:
        pairs = [(*split(first), trail[0]), (*split(second), trail[1])]
    total = None
    for high, low, right in pairs:
        right_high, right_low = split(right)
        both = dot16(jnp.concatenate([high, low], axis=0), right_high)
        term = both[: 2 * observers] + both[2 * observers :] + dot16(high, right_low)
        total = term if total is None else total + term
    extra = sent.shape[3] - n
    if extra:
        relative = jnp.where(index < half, 2 * index + 1, 2 * (index - half))
        target = row ^ relative
        sums = jnp.sum(x, axis=1, keepdims=True)
        partial = currents[0:1] * sums[0] - currents[1:2] * sums[1]
        ids = (target * cols + col) * PATCH_DEV + lax.broadcasted_iota(jnp.int32, (observers, depth), 0)
        found = jnp.where(owner[...] == ids, partial, 0.0)
        gradient = jnp.broadcast_to(jnp.sum(found, axis=1, keepdims=True), (observers, extra))

    def put(ref):
        ref[0, 0, :, 0:n] = total[:observers]
        ref[0, 1, :, 0:n] = total[observers:]
        if extra:
            ref[0, 0, :, n:] = gradient
            ref[0, 1, :, n:] = gradient

    @pl.when(index < half)
    def _():
        put(sent)

    @pl.when(index >= half)
    def _():
        put(kept)


def trail_product(flags, x_in, x_own, currents, owner, trail, chunk, chunks, devices, cols, members):
    depth = trail.shape[1]
    observers = x_own.shape[1]
    columns = trail.shape[2] // devices // chunks
    half = devices // 2
    extra = LANES if chunk == 0 else 0

    def place(i, flags):
        relative = jnp.where(i < half, 2 * i + 1, 2 * (i - half))
        return 0, 0, (flags[0] ^ relative) * chunks + chunk

    def full(a):
        return pl.BlockSpec(a.shape, lambda i, flags: (0,) * a.ndim)

    out = jax.ShapeDtypeStruct((half, 2, observers, columns + extra), jnp.float32)
    block = (1, 2, observers, columns + extra)
    return pl.pallas_call(
        functools.partial(trail_kernel, members, devices, cols),
        grid_spec=pltpu.PrefetchScalarGridSpec(
            num_scalar_prefetch=1,
            grid=(devices,),
            in_specs=[
                full(x_in),
                full(x_own),
                full(currents),
                full(owner),
                pl.BlockSpec((2, depth, columns), place),
            ],
            out_specs=[
                pl.BlockSpec(block, lambda i, flags: (jnp.minimum(i, half - 1), 0, 0, 0)),
                pl.BlockSpec(block, lambda i, flags: (jnp.maximum(i - half, 0), 0, 0, 0)),
            ],
        ),
        out_shape=[out, out],
        cost_estimate=pl.CostEstimate(
            flops=12 * observers * depth * columns * devices,
            bytes_accessed=4 * 2 * depth * columns * devices,
            transcendentals=0,
        ),
    )(flags, x_in, x_own, currents, owner, trail)


def on_device(upper_block, block_inverse, panel_rhs, upper_trail, trail_rhs, currents, owner):
    rows = lax.axis_size("row")
    cols = lax.axis_size("col")
    row = lax.axis_index("row")
    col = lax.axis_index("col")
    width = block_inverse.shape[1]
    quarter = upper_block.shape[2]
    observers = panel_rhs.shape[1]
    members = rows // cols
    bits = rows.bit_length() - 1

    def flat(r, c):
        return r * cols + c

    def leader(k):
        return flat(members * k + members - 1, k)

    def send(value, pairs):
        return lax.ppermute(value, ("row", "col"), pairs)

    rhs, inverse, inside = [], [], []
    for t in range(members - 1):
        pairs = [(flat(members * k + t, k), leader(k)) for k in range(cols)]
        inside.append(send(upper_block, pairs))
        inverse.append(send(block_inverse, pairs))
        rhs.append(send(panel_rhs, pairs))
    rhs.append(panel_rhs)
    inverse.append(block_inverse)
    pieces = []
    for d in range(1, cols):
        for t in range(members):
            pieces.append(send(upper_block, [(flat(members * (k - d) + t, k), leader(k)) for k in range(d, cols)]))

    earlier = []
    results = []
    for step in range(cols):
        used = pieces[: step * members]
        message = pl.pallas_call(
            functools.partial(step_kernel, step, members, width),
            out_shape=whole((2 * step + 2, observers, quarter)),
        )(*rhs, *inverse, *inside, *earlier, *used)
        results.append(message[2 * step : 2 * step + 2])
        if step + 1 < cols:
            earlier = [send(message, [(leader(step), leader(step + 1))])]

    mine = results[0]
    for k in range(1, cols):
        mine = jnp.where(col == k, results[k], mine)
    at_leader = mine
    for s in range(1, cols):
        pairs = [(leader(k), flat(members * k + members - 1, (k + s) % cols)) for k in range(cols)]
        arrived = send(at_leader, pairs)
        mine = jnp.where((row // members + s) % cols == col, arrived, mine)
    own = mine[:, :, (members - 1) * width :]
    passed = jnp.zeros_like(own)
    for t in range(members - 1):
        pairs = [(members * k + members - 1, members * k + t) for k in range(cols)]
        arrived = lax.ppermute(mine[:, :, t * width : (t + 1) * width], "row", pairs)
        passed = arrived if members == 2 else jnp.where(row % members == t, arrived, passed)
    last = (row % members == members - 1).astype(jnp.int32)
    solved = jnp.where(last == 1, own, passed)

    flags = jnp.stack([row.astype(jnp.int32), col.astype(jnp.int32), last])
    owner_row = owner.reshape(1, width)
    columns = upper_trail.shape[2] // rows // CHUNKS
    pieces_out, gradient = [], None
    for chunk in range(CHUNKS):
        sent, kept = trail_product(
            flags, passed, own, currents, owner_row, upper_trail, chunk, CHUNKS, rows, cols, members
        )
        arrived = lax.ppermute(sent, "row", [(i, i ^ 1) for i in range(rows)])
        summed = kept + arrived
        shape = (2,) * (bits - 1)
        parts = []
        for part in range(2):
            value = summed[:, part]
            if part == 1:
                value = value[:, :, :columns]
            value = value.reshape(shape + value.shape[1:])
            left = list(range(bits - 1, 0, -1))
            order = list(range(1, bits)) if part == 0 else list(range(bits - 1, 0, -1))
            for bit in order:
                value = halve(value, left.index(bit), bit, rows)
                left.remove(bit)
            parts.append(value)
        if chunk == 0:
            gradient = parts[0][:PATCH_DEV, columns]
        pieces_out.append(jnp.stack([parts[0][:, :columns], parts[1]]))
    updated = trail_rhs - jnp.concatenate(pieces_out, axis=2)
    return solved, updated, gradient


def solution(mesh):
    in_specs = (
        P(None, "row", "col"),
        P(None, "row", None),
        P(None, None, "row"),
        P(None, "row", "col"),
        P(None, None, ("col", "row")),
        P(None, "row"),
        P("row"),
    )
    out_specs = (P(None, None, "row"), P(None, None, ("col", "row")), P(("row", "col")))
    return jax.shard_map(
        on_device, mesh=mesh, in_specs=in_specs, out_specs=out_specs, check_vma=False
    )
```

```python
import functools

import jax
import jax.numpy as jnp
from jax import lax
from jax.experimental import pallas as pl
from jax.experimental.pallas import tpu as pltpu
from jax.sharding import PartitionSpec as P


PATCH_DEV = 4
LANES = 128
CHUNKS = 2


def dot16(first, second):
    return jnp.dot(first, second, preferred_element_type=jnp.float32)


def split(x):
    high = x.astype(jnp.bfloat16)
    return high, (x - high.astype(jnp.float32)).astype(jnp.bfloat16)


def stacked(left):
    first = jnp.concatenate([left[0], left[1]], axis=0)
    second = jnp.concatenate([left[1], -left[0]], axis=0)
    return first, second


def product(left, right):
    depth, n = left.shape[2], right.shape[2]
    first, second = stacked(left)
    rows = first.shape[0]
    if depth % LANES == 0:
        pairs = [(jnp.concatenate([first, second], axis=1), right.reshape(2 * depth, n))]
    else:
        pairs = [(first, right[0]), (second, right[1])]
    total = None
    for x, y in pairs:
        x_high, x_low = split(x)
        y_high, y_low = split(y)
        both = dot16(jnp.concatenate([x_high, x_low], axis=0), y_high)
        term = both[:rows] + both[rows:] + dot16(x_high, y_low)
        total = term if total is None else total + term
    return total


VMEM = pl.BlockSpec(memory_space=pltpu.VMEM)
ANY = pl.BlockSpec(memory_space=pl.ANY)


def local_call(kernel, outs, near, far=(), scratch=(), limit=16 << 20, far_outs=()):
    near = [pltpu.with_memory_space_constraint(a, pltpu.VMEM) for a in near]
    far = [pltpu.with_memory_space_constraint(a, pltpu.HBM) for a in far]
    return pl.pallas_call(
        kernel,
        in_specs=[VMEM] * len(near) + [ANY] * len(far),
        out_specs=[VMEM] * len(outs) + [ANY] * len(far_outs),
        out_shape=[pltpu.VMEM(shape, dtype) for shape, dtype in outs]
        + [pltpu.HBM(shape, dtype) for shape, dtype in far_outs],
        scratch_shapes=scratch,
        compiler_params=pltpu.CompilerParams(vmem_limit_bytes=limit),
    )(*near, *far)


def load_kernel(count, *refs):
    sources, targets, sems = refs[:count], refs[count : 2 * count], refs[2 * count]
    copies = [pltpu.make_async_copy(a, b, sems.at[i]) for i, (a, b) in enumerate(zip(sources, targets))]
    for copy in copies:
        copy.start()
    for copy in copies:
        copy.wait()


def after(value, other):
    return lax.optimization_barrier((value, other))[0]


def step_kernel(step, groups, members, width, *refs):
    refs = list(refs)
    out = refs.pop()
    rhs = [refs.pop(0) for _ in range(members)]
    inverse = [refs.pop(0) for _ in range(members)]
    inside = [refs.pop(0) for _ in range(members - 1)]
    earlier = refs.pop(0) if step else None
    pieces = [refs.pop(0) for _ in range(step * members)]
    results = refs
    observers = rhs[0].shape[1]
    final = step + 1 == groups
    row, col = lax.axis_index("row"), lax.axis_index("col")

    @pl.when((col == step) & (row == members * step + members - 1))
    def _():
        held = None
        for group in range(step):
            for t in range(members):
                x = earlier[2 * group : 2 * group + 2, :, t * width : (t + 1) * width]
                term = product(x, pieces[(step - group - 1) * members + t][...])
                held = term if held is None else held + term
        solved = []
        for b in range(members):
            residual = jnp.concatenate([rhs[b][0], rhs[b][1]], axis=0)
            if held is not None:
                residual = residual - held[:, b * width : (b + 1) * width]
            for a in range(b):
                residual = residual - product(solved[a], inside[a][:, :, b * width : (b + 1) * width])
            value = product(residual.reshape(2, observers, width), inverse[b][...])
            solved.append(value.reshape(2, observers, width))
        base = 0
        if not final:
            if step:
                out[0 : 2 * step] = earlier[...]
            base = 2 * step
        for b in range(members):
            out[base : base + 2, :, b * width : (b + 1) * width] = solved[b]

    if final:
        for k in range(step):
            @pl.when(col == k)
            def _(k=k):
                out[...] = results[k][2 * k : 2 * k + 2]


def merge_kernel(members, *refs):
    outs = refs[-members:]
    sources = refs[:-members]
    cols = len(sources)
    width = outs[0].shape[2]
    group, col = lax.div(lax.axis_index("row"), members), lax.axis_index("col")
    for s, source in enumerate(sources):
        @pl.when(lax.rem(group + s, cols) == col)
        def _(source=source):
            for t in range(members):
                outs[t][...] = source[:, :, t * width : (t + 1) * width]


def prepare_kernel(chunk, chunks, trail, high, low, room, sems):
    devices, columns = room.shape[0], room.shape[3]
    copies = []
    for i in range(devices):
        start = (i * chunks + chunk) * columns
        copies.append(pltpu.make_async_copy(trail.at[:, :, start : start + columns], room.at[i], sems.at[i]))
        copies[-1].start()
    for i in range(devices):
        copies[i].wait()
        for part in range(2):
            depth = room.shape[2]
            a, b = split(room[i, part])
            high[i, part * depth : (part + 1) * depth] = a
            low[i, part * depth : (part + 1) * depth] = b


def trail_kernel(chunk, chunks, cols, ready, members, currents, owner, *refs):
    row = lax.axis_index("row")
    if ready:
        candidates, refs = refs[:members], refs[members:]
        high, low, x, sent_a, sent_b, kept_a, kept_b, solved, sem = refs
        for t in range(members):
            @pl.when(lax.rem(row, members) == t)
            def _(t=t):
                x[...] = candidates[t][...]
        out = pltpu.make_async_copy(x, solved, sem)
        out.start()
    else:
        x, refs = refs[0], refs[1:]
    observers, depth = x.shape[1], x.shape[2]
    if ready:
        devices, columns = high.shape[0], high.shape[2]
    else:
        trail, sent_a, sent_b, kept_a, kept_b, room, sems = refs
        devices, columns = room.shape[0], room.shape[3]
    half = devices // 2
    targets = [row ^ (2 * (i % half) + (1 if i < half else 0)) for i in range(devices)]
    copies = []
    if not ready:
        for i, target in enumerate(targets):
            start = pl.multiple_of((target * chunks + chunk) * columns, LANES)
            copies.append(pltpu.make_async_copy(trail.at[:, :, pl.ds(start, columns)], room.at[i], sems.at[i]))
            copies[-1].start()
    first, second = stacked(x[...])
    if depth % LANES == 0:
        lefts = [split(jnp.concatenate([first, second], axis=1))]
    else:
        lefts = [split(first), split(second)]
    lefts = [(a, jnp.concatenate([a, b], axis=0)) for a, b in lefts]
    share = 2 * depth // len(lefts)
    extra = kept_a.shape[2] - columns
    if extra:
        col = lax.axis_index("col")
        sums = jnp.sum(x[...], axis=1, keepdims=True)
        partial = currents[0:1] * sums[0] - currents[1:2] * sums[1]
        patch = lax.broadcasted_iota(jnp.int32, (observers, depth), 0)
    for i, target in enumerate(targets):
        e = i % half
        ref_a, ref_b = (sent_a, sent_b) if i < half else (kept_a, kept_b)
        total = None
        if not ready:
            copies[i].wait()
            whole = room[i].reshape(2 * depth, columns)
        for j, (left, pair) in enumerate(lefts):
            place = slice(j * share, (j + 1) * share)
            if ready:
                right_high, right_low = high[target, place], low[target, place]
            else:
                right_high, right_low = split(whole[place])
            both = dot16(pair, right_high)
            term = both[: 2 * observers] + both[2 * observers :] + dot16(left, right_low)
            total = term if total is None else total + term
        ref_a[e, :, 0:columns] = total[:observers]
        ref_b[e] = total[observers:]
        if extra:
            found = jnp.where(owner[...] == patch + (target * cols + col) * PATCH_DEV, partial, 0.0)
            gradient = jnp.sum(found, axis=1, keepdims=True)
            ref_a[e, :, columns:] = jnp.broadcast_to(gradient, (observers, extra))
    if ready:
        out.wait()


def halve(values, axis, bit, rows):
    low = lax.index_in_dim(values, 0, axis, keepdims=False)
    high = lax.index_in_dim(values, 1, axis, keepdims=False)
    arrived = lax.ppermute(high, "row", [(i, i ^ (1 << bit)) for i in range(rows)])
    return low + arrived


def on_device(upper_block, block_inverse, panel_rhs, upper_trail, trail_rhs, currents, owner):
    rows = lax.axis_size("row")
    cols = lax.axis_size("col")
    width = block_inverse.shape[1]
    quarter = upper_block.shape[2]
    observers = panel_rhs.shape[1]
    members = rows // cols
    bits = rows.bit_length() - 1

    def flat(r, c):
        return r * cols + c

    def leader(k):
        return flat(members * k + members - 1, k)

    def send(value, pairs):
        return lax.ppermute(value, ("row", "col"), pairs)

    pieces = []

    def above(d, source):
        for t in range(members):
            pairs = [(flat(members * (k - d) + t, k), leader(k)) for k in range(d, cols)]
            pieces.append(send(source, pairs))

    above(1, upper_block)
    rhs, inverse, inside = [], [], []
    for t in range(members - 1):
        turn = members - 1 - t
        pairs = [(i, i // members * members + (i + turn) % members) for i in range(rows)]
        rhs.append(lax.ppermute(panel_rhs, "row", pairs))
        inverse.append(lax.ppermute(block_inverse, "row", pairs))
        inside.append(lax.ppermute(upper_block, "row", pairs))
    owner_row = owner.reshape(1, width)
    loaded = [panel_rhs, block_inverse, currents, owner_row]
    panel_near, inverse_near, currents_near, owner_near = local_call(
        functools.partial(load_kernel, len(loaded)),
        [(a.shape, a.dtype) for a in loaded],
        [],
        loaded,
        [pltpu.SemaphoreType.DMA((len(loaded),))],
        limit=2 << 20,
    )
    rhs.append(panel_near)
    inverse.append(inverse_near)

    columns = upper_trail.shape[2] // rows // CHUNKS
    room = [pltpu.VMEM((rows, 2, width, columns), jnp.float32), pltpu.SemaphoreType.DMA((rows,))]
    earlier, messages = [], []
    for step in range(cols):
        final = step + 1 == cols
        shape = (2 if final else 2 * step + 2, observers, quarter)
        message = local_call(
            functools.partial(step_kernel, step, cols, members, width),
            [(shape, jnp.float32)],
            [*rhs, *inverse, *inside, *earlier, *pieces[: step * members], *(messages if final else [])],
        )[0]
        messages.append(message)
        if not final:
            earlier = [send(message, [(leader(step), leader(step + 1))])]
        if step + 2 < cols:
            above(step + 2, after(upper_block, message))
        if step == min(1, cols - 2):
            ready = local_call(
                functools.partial(prepare_kernel, 0, CHUNKS),
                [((rows, 2 * width, columns), jnp.bfloat16)] * 2,
                [],
                [after(upper_trail, message)],
                room,
            )

    arrived = [messages[-1]]
    for s in range(1, cols):
        pairs = [(leader(k), flat(members * k + members - 1, (k + s) % cols)) for k in range(cols)]
        arrived.append(send(messages[-1], pairs))
    parts = local_call(
        functools.partial(merge_kernel, members),
        [((2, observers, width), jnp.float32)] * members,
        arrived,
        limit=2 << 20,
    )
    candidates = []
    for t in range(members - 1):
        turn = t - (members - 1)
        pairs = [(i, i // members * members + (i + turn) % members) for i in range(rows)]
        candidates.append(lax.ppermute(parts[t], "row", pairs))
    candidates.append(parts[-1])

    half = rows // 2
    out_parts, gradient, factor, solved = [], None, None, None
    for chunk in range(CHUNKS):
        extra = LANES if chunk == 0 else 0
        real, imag = (half, observers, columns + extra), (half, observers, columns)
        results = local_call(
            functools.partial(trail_kernel, chunk, CHUNKS, cols, chunk == 0, members),
            [(a, jnp.float32) for a in ([candidates[0].shape] if chunk == 0 else []) + [real, imag, real, imag]],
            [currents_near, owner_near, *([*candidates, *ready] if chunk == 0 else [factor])],
            [] if chunk == 0 else [upper_trail],
            [pltpu.SemaphoreType.DMA] if chunk == 0 else room,
            far_outs=[(candidates[0].shape, jnp.float32)] if chunk == 0 else [],
        )
        if chunk == 0:
            factor, *results, solved = results
        parts = []
        for part in range(2):
            arrived = lax.ppermute(results[part], "row", [(i, i ^ 1) for i in range(rows)])
            value = results[2 + part] + arrived
            value = value.reshape((2,) * (bits - 1) + value.shape[1:])
            left = list(range(bits - 1, 0, -1))
            order = left[::-1] if part == 0 else left[:]
            for bit in order:
                value = halve(value, left.index(bit), bit, rows)
                left.remove(bit)
            parts.append(value)
        if extra:
            gradient = parts[0][:PATCH_DEV, columns]
        out_parts.append(jnp.stack([parts[0][:, :columns], parts[1]]))
    updated = trail_rhs - jnp.concatenate(out_parts, axis=2)
    return solved, updated, gradient


def solution(mesh):
    in_specs = (
        P(None, "row", "col"),
        P(None, "row", None),
        P(None, None, "row"),
        P(None, "row", "col"),
        P(None, None, ("col", "row")),
        P(None, "row"),
        P("row"),
    )
    out_specs = (P(None, None, "row"), P(None, None, ("col", "row")), P(("row", "col")))

    return jax.shard_map(on_device, mesh=mesh, in_specs=in_specs, out_specs=out_specs, check_vma=False)
```

```python
import functools

import jax
import jax.numpy as jnp
from jax import lax
from jax.experimental import pallas as pl
from jax.experimental.pallas import tpu as pltpu
from jax.sharding import PartitionSpec as P


PATCH_DEV = 4
LANES = 128
CHUNKS = 2


def dot16(first, second):
    return jnp.dot(first, second, preferred_element_type=jnp.float32)


def split(x):
    high = x.astype(jnp.bfloat16)
    return high, (x - high.astype(jnp.float32)).astype(jnp.bfloat16)


def stacked(left):
    first = jnp.concatenate([left[0], left[1]], axis=0)
    second = jnp.concatenate([left[1], -left[0]], axis=0)
    return first, second


def product(left, right):
    depth, n = left.shape[2], right.shape[2]
    first, second = stacked(left)
    rows = first.shape[0]
    if depth % LANES == 0:
        pairs = [(jnp.concatenate([first, second], axis=1), right.reshape(2 * depth, n))]
    else:
        pairs = [(first, right[0]), (second, right[1])]
    total = None
    for x, y in pairs:
        x_high, x_low = split(x)
        y_high, y_low = split(y)
        both = dot16(jnp.concatenate([x_high, x_low], axis=0), y_high)
        term = both[:rows] + both[rows:] + dot16(x_high, y_low)
        total = term if total is None else total + term
    return total


VMEM = pl.BlockSpec(memory_space=pltpu.VMEM)
ANY = pl.BlockSpec(memory_space=pl.ANY)


def local_call(kernel, outs, near, far=(), scratch=(), limit=16 << 20, far_outs=(), aliases=None):
    near = [pltpu.with_memory_space_constraint(a, pltpu.VMEM) for a in near]
    far = [pltpu.with_memory_space_constraint(a, pltpu.HBM) for a in far]
    return pl.pallas_call(
        kernel,
        in_specs=[VMEM] * len(near) + [ANY] * len(far),
        out_specs=[VMEM] * len(outs) + [ANY] * len(far_outs),
        out_shape=[pltpu.VMEM(shape, dtype) for shape, dtype in outs]
        + [pltpu.HBM(shape, dtype) for shape, dtype in far_outs],
        scratch_shapes=scratch,
        input_output_aliases=aliases or {},
        compiler_params=pltpu.CompilerParams(vmem_limit_bytes=limit),
    )(*near, *far)


def load_kernel(count, *refs):
    sources, targets, sems = refs[:count], refs[count : 2 * count], refs[2 * count]
    copies = [pltpu.make_async_copy(a, b, sems.at[i]) for i, (a, b) in enumerate(zip(sources, targets))]
    for copy in copies:
        copy.start()
    for copy in copies:
        copy.wait()


def after(value, other):
    return lax.optimization_barrier((value, other))[0]


def step_kernel(step, groups, members, width, *refs):
    refs = list(refs)
    out = refs.pop()
    rhs = [refs.pop(0) for _ in range(members)]
    inverse = [refs.pop(0) for _ in range(members)]
    inside = [refs.pop(0) for _ in range(members - 1)]
    earlier = refs.pop(0) if step else None
    pieces = [refs.pop(0) for _ in range(step * members)]
    results = refs
    observers = rhs[0].shape[1]
    final = step + 1 == groups
    row, col = lax.axis_index("row"), lax.axis_index("col")

    @pl.when((col == step) & (row == members * step + members - 1))
    def _():
        held = None
        for group in range(step):
            for t in range(members):
                x = earlier[2 * group : 2 * group + 2, :, t * width : (t + 1) * width]
                term = product(x, pieces[(step - group - 1) * members + t][...])
                held = term if held is None else held + term
        solved = []
        for b in range(members):
            residual = jnp.concatenate([rhs[b][0], rhs[b][1]], axis=0)
            if held is not None:
                residual = residual - held[:, b * width : (b + 1) * width]
            for a in range(b):
                residual = residual - product(solved[a], inside[a][:, :, b * width : (b + 1) * width])
            value = product(residual.reshape(2, observers, width), inverse[b][...])
            solved.append(value.reshape(2, observers, width))
        base = 0
        if not final:
            if step:
                out[0 : 2 * step] = earlier[...]
            base = 2 * step
        for b in range(members):
            out[base : base + 2, :, b * width : (b + 1) * width] = solved[b]

    if final:
        for k in range(step):
            @pl.when(col == k)
            def _(k=k):
                out[...] = results[k][2 * k : 2 * k + 2]


def merge_kernel(members, *refs):
    outs = refs[-members:]
    sources = refs[:-members]
    cols = len(sources)
    width = outs[0].shape[2]
    group, col = lax.div(lax.axis_index("row"), members), lax.axis_index("col")
    for s, source in enumerate(sources):
        @pl.when(lax.rem(group + s, cols) == col)
        def _(source=source):
            for t in range(members):
                outs[t][...] = source[:, :, t * width : (t + 1) * width]


def when_kernel(last, members, skip, kernel, *refs):
    inside = lax.axis_index("row") >= lax.axis_size("row") - members

    @pl.when(inside if last else jnp.logical_not(inside))
    def _():
        kernel(*refs[skip[0] : skip[1]], *refs[skip[2] :])


def prepare_kernel(chunk, chunks, trail, high, low, room, sems):
    devices, columns = room.shape[0], room.shape[3]
    copies = []
    for i in range(devices):
        start = (i * chunks + chunk) * columns
        copies.append(pltpu.make_async_copy(trail.at[:, :, start : start + columns], room.at[i], sems.at[i]))
        copies[-1].start()
    for i in range(devices):
        copies[i].wait()
        for part in range(2):
            depth = room.shape[2]
            a, b = split(room[i, part])
            high[i, part * depth : (part + 1) * depth] = a
            low[i, part * depth : (part + 1) * depth] = b


def trail_kernel(chunk, chunks, cols, ready, select, odds, members, currents, owner, *refs):
    row = lax.axis_index("row")
    refs = list(refs)
    candidates = [refs.pop(0) for _ in range(members if select else 1)]
    factors = [refs.pop(0) for _ in range(2 if ready else 1)]
    x = refs.pop(0) if select else candidates[0]
    outs = {odd: (refs.pop(0), refs.pop(0)) for odd in odds}
    if select:
        solved, sem = refs
        for t in range(members):
            @pl.when(lax.rem(row, members) == t)
            def _(t=t):
                x[...] = candidates[t][...]
        out = pltpu.make_async_copy(x, solved, sem)
        out.start()
    observers, depth = x.shape[1], x.shape[2]
    if ready:
        high, low = factors
        devices, columns = high.shape[0], high.shape[2]
    else:
        trail, (room, sems) = factors[0], refs
        devices, columns = room.shape[0], room.shape[3]
    half = devices // 2
    work = [(row ^ (2 * e + odd), e, odd) for odd in odds for e in range(half)]
    copies = []
    if not ready:
        for i, (target, _, _) in enumerate(work):
            start = pl.multiple_of((target * chunks + chunk) * columns, LANES)
            copies.append(pltpu.make_async_copy(trail.at[:, :, pl.ds(start, columns)], room.at[i], sems.at[i]))
            copies[-1].start()
    first, second = stacked(x[...])
    if depth % LANES == 0:
        lefts = [split(jnp.concatenate([first, second], axis=1))]
    else:
        lefts = [split(first), split(second)]
    lefts = [(a, jnp.concatenate([a, b], axis=0)) for a, b in lefts]
    share = 2 * depth // len(lefts)
    extra = outs[odds[0]][0].shape[2] - columns
    if extra:
        col = lax.axis_index("col")
        sums = jnp.sum(x[...], axis=1, keepdims=True)
        partial = currents[0:1] * sums[0] - currents[1:2] * sums[1]
        patch = lax.broadcasted_iota(jnp.int32, (observers, depth), 0)
    for i, (target, e, odd) in enumerate(work):
        ref_a, ref_b = outs[odd]
        total = None
        if not ready:
            copies[i].wait()
            whole = room[i].reshape(2 * depth, columns)
        for j, (left, pair) in enumerate(lefts):
            place = slice(j * share, (j + 1) * share)
            if ready:
                right_high, right_low = high[target, place], low[target, place]
            else:
                right_high, right_low = split(whole[place])
            both = dot16(pair, right_high)
            term = both[: 2 * observers] + both[2 * observers :] + dot16(left, right_low)
            total = term if total is None else total + term
        ref_a[e, :, 0:columns] = total[:observers]
        ref_b[e] = total[observers:]
        if extra:
            found = jnp.where(owner[...] == patch + (target * cols + col) * PATCH_DEV, partial, 0.0)
            gradient = jnp.sum(found, axis=1, keepdims=True)
            ref_a[e, :, columns:] = jnp.broadcast_to(gradient, (observers, extra))
    if select:
        out.wait()


def halve(values, axis, bit, rows):
    low = lax.index_in_dim(values, 0, axis, keepdims=False)
    high = lax.index_in_dim(values, 1, axis, keepdims=False)
    arrived = lax.ppermute(high, "row", [(i, i ^ (1 << bit)) for i in range(rows)])
    return low + arrived


def on_device(upper_block, block_inverse, panel_rhs, upper_trail, trail_rhs, currents, owner):
    rows = lax.axis_size("row")
    cols = lax.axis_size("col")
    width = block_inverse.shape[1]
    quarter = upper_block.shape[2]
    observers = panel_rhs.shape[1]
    members = rows // cols
    bits = rows.bit_length() - 1

    def flat(r, c):
        return r * cols + c

    def leader(k):
        return flat(members * k + members - 1, k)

    def send(value, pairs):
        return lax.ppermute(value, ("row", "col"), pairs)

    pieces = []

    def above(d, source):
        for t in range(members):
            pairs = [(flat(members * (k - d) + t, k), leader(k)) for k in range(d, cols)]
            pieces.append(send(source, pairs))

    above(1, upper_block)
    rhs, inverse, inside = [], [], []
    for t in range(members - 1):
        turn = members - 1 - t
        pairs = [(i, i // members * members + (i + turn) % members) for i in range(rows)]
        rhs.append(lax.ppermute(panel_rhs, "row", pairs))
        inverse.append(lax.ppermute(block_inverse, "row", pairs))
        inside.append(lax.ppermute(upper_block, "row", pairs))
    owner_row = owner.reshape(1, width)
    loaded = [panel_rhs, block_inverse, currents, owner_row]
    panel_near, inverse_near, currents_near, owner_near = local_call(
        functools.partial(load_kernel, len(loaded)),
        [(a.shape, a.dtype) for a in loaded],
        [],
        loaded,
        [pltpu.SemaphoreType.DMA((len(loaded),))],
        limit=2 << 20,
    )
    rhs.append(panel_near)
    inverse.append(inverse_near)

    columns = upper_trail.shape[2] // rows // CHUNKS
    room = [pltpu.VMEM((rows, 2, width, columns), jnp.float32), pltpu.SemaphoreType.DMA((rows,))]
    earlier, messages = [], []
    for step in range(cols):
        final = step + 1 == cols
        shape = (2 if final else 2 * step + 2, observers, quarter)
        message = local_call(
            functools.partial(step_kernel, step, cols, members, width),
            [(shape, jnp.float32)],
            [*rhs, *inverse, *inside, *earlier, *pieces[: step * members], *(messages if final else [])],
        )[0]
        messages.append(message)
        if not final:
            earlier = [send(message, [(leader(step), leader(step + 1))])]
        if step + 2 < cols:
            above(step + 2, after(upper_block, message))
        if step == min(1, cols - 2):
            ready = local_call(
                functools.partial(prepare_kernel, 0, CHUNKS),
                [((rows, 2 * width, columns), jnp.bfloat16)] * 2,
                [],
                [after(upper_trail, message)],
                room,
            )

    arrived = [messages[-1]]
    for s in range(1, cols):
        pairs = [(leader(k), flat(members * k + members - 1, (k + s) % cols)) for k in range(cols)]
        arrived.append(send(messages[-1], pairs))
    parts = local_call(
        functools.partial(merge_kernel, members),
        [((2, observers, width), jnp.float32)] * members,
        arrived,
        limit=2 << 20,
    )
    candidates = []
    for t in range(members - 1):
        turn = t - (members - 1)
        pairs = [(i, i // members * members + (i + turn) % members) for i in range(rows)]
        candidates.append(lax.ppermute(parts[t], "row", pairs))
    candidates.append(parts[-1])

    half = rows // 2
    out_parts, gradient, factor, solved = [], None, None, None
    small = [currents_near, owner_near]
    for chunk in range(CHUNKS):
        extra = LANES if chunk == 0 else 0
        shapes = [((half, observers, columns + extra), jnp.float32), ((half, observers, columns), jnp.float32)]

        def trail(select, odds, operands, far, scratch):
            return local_call(
                functools.partial(trail_kernel, chunk, CHUNKS, cols, chunk == 0, select, odds, members),
                ([(candidates[0].shape, jnp.float32)] if select else []) + shapes * len(odds),
                [*small, *operands],
                far,
                scratch,
                far_outs=[(candidates[0].shape, jnp.float32)] if select else [],
            )

        if chunk == 0:
            factor, *sent, solved = trail(True, (1,), [*candidates, *ready], [], [pltpu.SemaphoreType.DMA])
            kept = trail(False, (0,), [after(factor, sent[0]), *ready], [], [])
        else:
            kernel = functools.partial(trail_kernel, chunk, CHUNKS, cols, False, False, (1, 0), members)
            outs = shapes * 2
            operands = [*small, factor]
            count = len(operands)
            results = local_call(
                functools.partial(when_kernel, False, members, (0, count, count), kernel),
                outs,
                [*small, after(factor, kept[0])],
                [upper_trail],
                room,
            )
            total = count + len(outs)
            results = local_call(
                functools.partial(when_kernel, True, members, (0, count, total), kernel),
                outs,
                [*operands, *results],
                [upper_trail],
                room,
                aliases={count + i: i for i in range(len(outs))},
            )
            sent, kept = results[:2], results[2:]
        parts = []
        for part in range(2):
            arrived = lax.ppermute(sent[part], "row", [(i, i ^ 1) for i in range(rows)])
            value = kept[part] + arrived
            value = value.reshape((2,) * (bits - 1) + value.shape[1:])
            left = list(range(bits - 1, 0, -1))
            order = left[::-1] if part == 0 else left[:]
            for bit in order:
                value = halve(value, left.index(bit), bit, rows)
                left.remove(bit)
            parts.append(value)
        if extra:
            gradient = parts[0][:PATCH_DEV, columns]
        out_parts.append(jnp.stack([parts[0][:, :columns], parts[1]]))
    updated = trail_rhs - jnp.concatenate(out_parts, axis=2)
    return solved, updated, gradient


def solution(mesh):
    in_specs = (
        P(None, "row", "col"),
        P(None, "row", None),
        P(None, None, "row"),
        P(None, "row", "col"),
        P(None, None, ("col", "row")),
        P(None, "row"),
        P("row"),
    )
    out_specs = (P(None, None, "row"), P(None, None, ("col", "row")), P(("row", "col")))

    return jax.shard_map(on_device, mesh=mesh, in_specs=in_specs, out_specs=out_specs, check_vma=False)
```

```python
import functools

import jax
import jax.numpy as jnp
from jax import lax
from jax.experimental import pallas as pl
from jax.experimental.pallas import tpu as pltpu
from jax.sharding import PartitionSpec as P


PATCH_DEV = 4
LANES = 128
CHUNKS = 2


def dot16(first, second):
    return jnp.dot(first, second, preferred_element_type=jnp.float32)


def split(x):
    high = x.astype(jnp.bfloat16)
    return high, (x - high.astype(jnp.float32)).astype(jnp.bfloat16)


def stacked(left):
    first = jnp.concatenate([left[0], left[1]], axis=0)
    second = jnp.concatenate([left[1], -left[0]], axis=0)
    return first, second


def product(left, right):
    depth, n = left.shape[2], right.shape[2]
    first, second = stacked(left)
    rows = first.shape[0]
    if depth % LANES == 0:
        pairs = [(jnp.concatenate([first, second], axis=1), right.reshape(2 * depth, n))]
    else:
        pairs = [(first, right[0]), (second, right[1])]
    total = None
    for x, y in pairs:
        x_high, x_low = split(x)
        y_high, y_low = split(y)
        both = dot16(jnp.concatenate([x_high, x_low], axis=0), y_high)
        term = both[:rows] + both[rows:] + dot16(x_high, y_low)
        total = term if total is None else total + term
    return total


VMEM = pl.BlockSpec(memory_space=pltpu.VMEM)
ANY = pl.BlockSpec(memory_space=pl.ANY)


def local_call(kernel, outs, near, far=(), scratch=(), limit=16 << 20, far_outs=(), aliases=None):
    near = [pltpu.with_memory_space_constraint(a, pltpu.VMEM) for a in near]
    far = [pltpu.with_memory_space_constraint(a, pltpu.HBM) for a in far]
    return pl.pallas_call(
        kernel,
        in_specs=[VMEM] * len(near) + [ANY] * len(far),
        out_specs=[VMEM] * len(outs) + [ANY] * len(far_outs),
        out_shape=[pltpu.VMEM(shape, dtype) for shape, dtype in outs]
        + [pltpu.HBM(shape, dtype) for shape, dtype in far_outs],
        scratch_shapes=scratch,
        input_output_aliases=aliases or {},
        compiler_params=pltpu.CompilerParams(vmem_limit_bytes=limit),
    )(*near, *far)


def load_kernel(count, *refs):
    sources, targets, sems = refs[:count], refs[count : 2 * count], refs[2 * count]
    copies = [pltpu.make_async_copy(a, b, sems.at[i]) for i, (a, b) in enumerate(zip(sources, targets))]
    for copy in copies:
        copy.start()
    for copy in copies:
        copy.wait()


def after(value, other):
    return lax.optimization_barrier((value, other))[0]


def leads(group, members):
    return (lax.axis_index("col") == group) & (lax.axis_index("row") == members * group + members - 1)


def step_kernel(step, members, width, near, held, *refs):
    refs = list(refs)
    out = refs.pop()
    rhs = [refs.pop(0) for _ in range(members)]
    inverse = [refs.pop(0) for _ in range(members)]
    inside = [refs.pop(0) for _ in range(members - 1)]
    terms = [refs.pop(0) for _ in range(held)]
    earlier = [(refs.pop(0), [refs.pop(0) for _ in range(members)]) for _ in range(near)]
    results = refs
    observers = rhs[0].shape[1]

    @pl.when(leads(step, members))
    def _():
        total = None
        for x, pieces in earlier:
            for t in range(members):
                term = product(x[:, :, t * width : (t + 1) * width], pieces[t][...])
                total = term if total is None else total + term
        for ref in terms:
            term = ref[...].reshape(2 * observers, members * width)
            total = term if total is None else total + term
        solved = []
        for b in range(members):
            residual = jnp.concatenate([rhs[b][0], rhs[b][1]], axis=0)
            if total is not None:
                residual = residual - total[:, b * width : (b + 1) * width]
            for a in range(b):
                residual = residual - product(solved[a], inside[a][:, :, b * width : (b + 1) * width])
            value = product(residual.reshape(2, observers, width), inverse[b][...])
            solved.append(value.reshape(2, observers, width))
            out[:, :, b * width : (b + 1) * width] = solved[b]

    for k, result in enumerate(results):
        @pl.when(leads(k, members))
        def _(result=result):
            out[...] = result[...]


def held_kernel(group, targets, members, width, *refs):
    out = refs[-1]
    pieces = refs[-1 - members : -1]
    row, col = lax.axis_index("row"), lax.axis_index("col")
    for k, x in zip(targets, refs):
        @pl.when((row == members * group + members - 1) & (col == k))
        def _(x=x):
            total = None
            for t in range(members):
                term = product(x[:, :, t * width : (t + 1) * width], pieces[t][...])
                total = term if total is None else total + term
            out[...] = total.reshape(out.shape)


def merge_kernel(members, sources, *refs):
    outs = refs[-members:]
    width = outs[0].shape[2]
    group, col = lax.div(lax.axis_index("row"), members), lax.axis_index("col")
    for source, places in zip(refs, sources):
        for i, k in places:
            @pl.when((group == i) & (col == k))
            def _(source=source):
                for t in range(members):
                    outs[t][...] = source[:, :, t * width : (t + 1) * width]


def when_kernel(last, members, skip, kernel, *refs):
    inside = lax.axis_index("row") >= lax.axis_size("row") - members

    @pl.when(inside if last else jnp.logical_not(inside))
    def _():
        kernel(*refs[skip[0] : skip[1]], *refs[skip[2] :])


def prepare_kernel(chunk, chunks, members, busy, late, skip, *refs):
    trail, high, low, room, sems = refs[skip:]
    devices, columns = room.shape[0], room.shape[3]
    waits = jnp.bool_(False)
    for k in busy:
        waits = waits | leads(k, members)

    @pl.when(waits if late else jnp.logical_not(waits))
    def _():
        copies = []
        for i in range(devices):
            start = (i * chunks + chunk) * columns
            copies.append(pltpu.make_async_copy(trail.at[:, :, start : start + columns], room.at[i], sems.at[i]))
            copies[-1].start()
        for i in range(devices):
            copies[i].wait()
            for part in range(2):
                depth = room.shape[2]
                a, b = split(room[i, part])
                high[i, part * depth : (part + 1) * depth] = a
                low[i, part * depth : (part + 1) * depth] = b


def trail_kernel(chunk, chunks, cols, ready, select, odds, members, currents, owner, *refs):
    row = lax.axis_index("row")
    refs = list(refs)
    candidates = [refs.pop(0) for _ in range(members if select else 1)]
    factors = [refs.pop(0) for _ in range(2 if ready else 1)]
    x = refs.pop(0) if select else candidates[0]
    outs = {odd: (refs.pop(0), refs.pop(0)) for odd in odds}
    if select:
        solved, sem = refs
        for t in range(members):
            @pl.when(lax.rem(row, members) == t)
            def _(t=t):
                x[...] = candidates[t][...]
        out = pltpu.make_async_copy(x, solved, sem)
        out.start()
    observers, depth = x.shape[1], x.shape[2]
    if ready:
        high, low = factors
        devices, columns = high.shape[0], high.shape[2]
    else:
        trail, (room, sems) = factors[0], refs
        devices, columns = room.shape[0], room.shape[3]
    half = devices // 2
    work = [(row ^ (2 * e + odd), e, odd) for odd in odds for e in range(half)]
    copies = []
    if not ready:
        for i, (target, _, _) in enumerate(work):
            start = pl.multiple_of((target * chunks + chunk) * columns, LANES)
            copies.append(pltpu.make_async_copy(trail.at[:, :, pl.ds(start, columns)], room.at[i], sems.at[i]))
            copies[-1].start()
    first, second = stacked(x[...])
    if depth % LANES == 0:
        lefts = [split(jnp.concatenate([first, second], axis=1))]
    else:
        lefts = [split(first), split(second)]
    lefts = [(a, jnp.concatenate([a, b], axis=0)) for a, b in lefts]
    share = 2 * depth // len(lefts)
    extra = outs[odds[0]][0].shape[2] - columns
    if extra:
        col = lax.axis_index("col")
        sums = jnp.sum(x[...], axis=1, keepdims=True)
        partial = currents[0:1] * sums[0] - currents[1:2] * sums[1]
        patch = lax.broadcasted_iota(jnp.int32, (observers, depth), 0)
    for i, (target, e, odd) in enumerate(work):
        ref_a, ref_b = outs[odd]
        total = None
        if not ready:
            copies[i].wait()
            whole = room[i].reshape(2 * depth, columns)
        for j, (left, pair) in enumerate(lefts):
            place = slice(j * share, (j + 1) * share)
            if ready:
                right_high, right_low = high[target, place], low[target, place]
            else:
                right_high, right_low = split(whole[place])
            both = dot16(pair, right_high)
            term = both[: 2 * observers] + both[2 * observers :] + dot16(left, right_low)
            total = term if total is None else total + term
        ref_a[e, :, 0:columns] = total[:observers]
        ref_b[e] = total[observers:]
        if extra:
            found = jnp.where(owner[...] == patch + (target * cols + col) * PATCH_DEV, partial, 0.0)
            gradient = jnp.sum(found, axis=1, keepdims=True)
            ref_a[e, :, columns:] = jnp.broadcast_to(gradient, (observers, extra))
    if select:
        out.wait()


def halve(values, axis, bit, rows):
    low = lax.index_in_dim(values, 0, axis, keepdims=False)
    high = lax.index_in_dim(values, 1, axis, keepdims=False)
    arrived = lax.ppermute(high, "row", [(i, i ^ (1 << bit)) for i in range(rows)])
    return low + arrived


def on_device(upper_block, block_inverse, panel_rhs, upper_trail, trail_rhs, currents, owner):
    rows = lax.axis_size("row")
    cols = lax.axis_size("col")
    width = block_inverse.shape[1]
    quarter = upper_block.shape[2]
    observers = panel_rhs.shape[1]
    members = rows // cols
    bits = rows.bit_length() - 1

    def flat(r, c):
        return r * cols + c

    def leader(k):
        return flat(members * k + members - 1, k)

    def send(value, pairs):
        return lax.ppermute(value, ("row", "col"), pairs)

    def near(k):
        return [g for g in ([k - 1, k - 2] if k % 2 and k > 1 else [k - 1]) if g >= 0]

    def far(g):
        return [k for k in range(g + 2, cols) if g not in near(k)]

    pieces = {}

    def bring(number):
        for t in range(members):
            moves = [(k, near(k)[number - 1]) for k in range(1, cols) if len(near(k)) >= number]
            if moves:
                arrived = send(upper_block, [(flat(members * g + t, k), leader(k)) for k, g in moves])
                for k, g in moves:
                    pieces[k, g, t] = arrived

    bring(1)
    rhs, inverse, inside = [], [], []
    for t in range(members - 1):
        turn = members - 1 - t
        pairs = [(i, i // members * members + (i + turn) % members) for i in range(rows)]
        rhs.append(lax.ppermute(panel_rhs, "row", pairs))
        inverse.append(lax.ppermute(block_inverse, "row", pairs))
        inside.append(lax.ppermute(upper_block, "row", pairs))
    bring(2)
    owner_row = owner.reshape(1, width)
    loaded = [panel_rhs, block_inverse, currents, owner_row, upper_block]
    panel_near, inverse_near, currents_near, owner_near, upper_near = local_call(
        functools.partial(load_kernel, len(loaded)),
        [(a.shape, a.dtype) for a in loaded],
        [],
        loaded,
        [pltpu.SemaphoreType.DMA((len(loaded),))],
        limit=2 << 20,
    )
    rhs.append(panel_near)
    inverse.append(inverse_near)
    upper_rows = [*inside, upper_near]

    columns = upper_trail.shape[2] // rows // CHUNKS
    room = [pltpu.VMEM((rows, 2, width, columns), jnp.float32), pltpu.SemaphoreType.DMA((rows,))]
    part = (2, observers, quarter)
    results, passed, held, early = [], {}, {}, {}
    arrived, sources = [], []

    def spread(value, places):
        arrived.append(send(value, [(leader(g), flat(members * g + members - 1, k)) for g, k in places]))
        sources.append(places)

    busy = []
    ready = []

    def prepare(place, source):
        nonlocal ready
        ready = local_call(
            functools.partial(prepare_kernel, 0, CHUNKS, members, busy, place == 1, len(ready)),
            [((rows, 2 * width, columns), jnp.bfloat16)] * 2,
            ready,
            [source],
            room,
            aliases={i: i for i in range(len(ready))},
        )

    for step in range(cols):
        final = step + 1 == cols
        terms = [held[g] for g in range(step) if step in far(g)]
        factors = []
        for g in near(step):
            factors += [passed[g, step], *(pieces[step, g, t] for t in range(members))]
        result = local_call(
            functools.partial(step_kernel, step, members, width, len(near(step)), len(terms)),
            [(part, jnp.float32)],
            [*rhs, *inverse, *inside, *terms, *factors, *(results if step == cols - 2 else [])],
        )[0]
        results.append(result)
        if not final:
            passed[step, step + 1] = send(result, [(leader(step), leader(step + 1))])
        if step + 2 < cols and step in near(step + 2):
            passed[step, step + 2] = send(result, [(leader(step), leader(step + 2))])
        for k in far(step):
            early[step, k] = send(result, [(leader(step), flat(members * step + members - 1, k))])
        if far(step):
            term = local_call(
                functools.partial(held_kernel, step, far(step), members, width),
                [(part, jnp.float32)],
                [*(early[step, k] for k in far(step)), *upper_rows],
            )[0]
            held[step] = send(term, [(flat(members * step + members - 1, k), leader(k)) for k in far(step)])
        if step == min(1, cols - 2):
            prepare(0, after(upper_trail, result))
        if step == cols - 2:
            arrived += [result, *early.values()]
            sources += [[(k, k) for k in range(cols - 1)], *([place] for place in early)]
            for s in range(1, cols):
                places = [(k, (k + s) % cols) for k in range(cols - 1)]
                spread(result, [place for place in places if place not in early])

    arrived += [results[-1]]
    sources += [[(cols - 1, cols - 1)]]
    for s in range(1, cols):
        spread(results[-1], [(cols - 1, (cols - 1 + s) % cols)])
    parts = local_call(
        functools.partial(merge_kernel, members, sources),
        [((2, observers, width), jnp.float32)] * members,
        arrived,
        limit=2 << 20,
    )
    candidates = []
    for t in range(members - 1):
        turn = t - (members - 1)
        pairs = [(i, i // members * members + (i + turn) % members) for i in range(rows)]
        candidates.append(lax.ppermute(parts[t], "row", pairs))
    candidates.append(parts[-1])

    half = rows // 2
    out_parts, gradient, factor, solved = [], None, None, None
    small = [currents_near, owner_near]
    for chunk in range(CHUNKS):
        extra = LANES if chunk == 0 else 0
        shapes = [((half, observers, columns + extra), jnp.float32), ((half, observers, columns), jnp.float32)]

        def trail(select, odds, operands, far, scratch):
            return local_call(
                functools.partial(trail_kernel, chunk, CHUNKS, cols, chunk == 0, select, odds, members),
                ([(candidates[0].shape, jnp.float32)] if select else []) + shapes * len(odds),
                [*small, *operands],
                far,
                scratch,
                far_outs=[(candidates[0].shape, jnp.float32)] if select else [],
            )

        if chunk == 0:
            factor, *sent, solved = trail(True, (1,), [*candidates, *ready], [], [pltpu.SemaphoreType.DMA])
            kept = trail(False, (0,), [after(factor, sent[0]), *ready], [], [])
        else:
            kernel = functools.partial(trail_kernel, chunk, CHUNKS, cols, False, False, (1, 0), members)
            outs = shapes * 2
            operands = [*small, factor]
            count = len(operands)
            results = local_call(
                functools.partial(when_kernel, False, members, (0, count, count), kernel),
                outs,
                [*small, after(factor, kept[0])],
                [upper_trail],
                room,
            )
            total = count + len(outs)
            results = local_call(
                functools.partial(when_kernel, True, members, (0, count, total), kernel),
                outs,
                [*operands, *results],
                [upper_trail],
                room,
                aliases={count + i: i for i in range(len(outs))},
            )
            sent, kept = results[:2], results[2:]
        parts = []
        for part in range(2):
            arrived = lax.ppermute(sent[part], "row", [(i, i ^ 1) for i in range(rows)])
            value = kept[part] + arrived
            value = value.reshape((2,) * (bits - 1) + value.shape[1:])
            left = list(range(bits - 1, 0, -1))
            order = left[::-1] if part == 0 else left[:]
            for bit in order:
                value = halve(value, left.index(bit), bit, rows)
                left.remove(bit)
            parts.append(value)
        if extra:
            gradient = parts[0][:PATCH_DEV, columns]
        out_parts.append(jnp.stack([parts[0][:, :columns], parts[1]]))
    updated = trail_rhs - jnp.concatenate(out_parts, axis=2)
    return solved, updated, gradient


def solution(mesh):
    in_specs = (
        P(None, "row", "col"),
        P(None, "row", None),
        P(None, None, "row"),
        P(None, "row", "col"),
        P(None, None, ("col", "row")),
        P(None, "row"),
        P("row"),
    )
    out_specs = (P(None, None, "row"), P(None, None, ("col", "row")), P(("row", "col")))

    return jax.shard_map(on_device, mesh=mesh, in_specs=in_specs, out_specs=out_specs, check_vma=False)
```

```python
import functools

import jax
import jax.numpy as jnp
from jax import lax
from jax.experimental import pallas as pl
from jax.experimental.pallas import tpu as pltpu
from jax.sharding import PartitionSpec as P


PATCH_DEV = 4
LANES = 128
CHUNKS = 2


def dot16(first, second):
    return jnp.dot(first, second, preferred_element_type=jnp.float32)


def split(x):
    high = x.astype(jnp.bfloat16)
    return high, (x - high.astype(jnp.float32)).astype(jnp.bfloat16)


def stacked(left):
    first = jnp.concatenate([left[0], left[1]], axis=0)
    second = jnp.concatenate([left[1], -left[0]], axis=0)
    return first, second


def product(left, right):
    depth, n = left.shape[2], right.shape[2]
    first, second = stacked(left)
    rows = first.shape[0]
    if depth % LANES == 0:
        pairs = [(jnp.concatenate([first, second], axis=1), right.reshape(2 * depth, n))]
    else:
        pairs = [(first, right[0]), (second, right[1])]
    total = None
    for x, y in pairs:
        x_high, x_low = split(x)
        y_high, y_low = split(y)
        both = dot16(jnp.concatenate([x_high, x_low], axis=0), y_high)
        term = both[:rows] + both[rows:] + dot16(x_high, y_low)
        total = term if total is None else total + term
    return total


VMEM = pl.BlockSpec(memory_space=pltpu.VMEM)
ANY = pl.BlockSpec(memory_space=pl.ANY)


def local_call(kernel, outs, near, far=(), scratch=(), limit=16 << 20, far_outs=(), aliases=None):
    near = [pltpu.with_memory_space_constraint(a, pltpu.VMEM) for a in near]
    far = [pltpu.with_memory_space_constraint(a, pltpu.HBM) for a in far]
    return pl.pallas_call(
        kernel,
        in_specs=[VMEM] * len(near) + [ANY] * len(far),
        out_specs=[VMEM] * len(outs) + [ANY] * len(far_outs),
        out_shape=[pltpu.VMEM(shape, dtype) for shape, dtype in outs]
        + [pltpu.HBM(shape, dtype) for shape, dtype in far_outs],
        scratch_shapes=scratch,
        input_output_aliases=aliases or {},
        compiler_params=pltpu.CompilerParams(vmem_limit_bytes=limit),
    )(*near, *far)


def load_kernel(count, *refs):
    sources, targets, sems = refs[:count], refs[count : 2 * count], refs[2 * count]
    copies = [pltpu.make_async_copy(a, b, sems.at[i]) for i, (a, b) in enumerate(zip(sources, targets))]
    for copy in copies:
        copy.start()
    for copy in copies:
        copy.wait()


def after(value, other):
    return lax.optimization_barrier((value, other))[0]


def leads(group, members):
    return (lax.axis_index("col") == group) & (lax.axis_index("row") == members * group + members - 1)


def step_kernel(step, members, width, near, held, *refs):
    refs = list(refs)
    out = refs.pop()
    rhs = [refs.pop(0) for _ in range(members)]
    inverse = [refs.pop(0) for _ in range(members)]
    inside = [refs.pop(0) for _ in range(members - 1)]
    terms = [refs.pop(0) for _ in range(held)]
    earlier = [(refs.pop(0), [refs.pop(0) for _ in range(members)]) for _ in range(near)]
    results = refs
    observers = rhs[0].shape[1]

    @pl.when(leads(step, members))
    def _():
        total = None
        for x, pieces in earlier:
            for t in range(members):
                term = product(x[:, :, t * width : (t + 1) * width], pieces[t][...])
                total = term if total is None else total + term
        for ref in terms:
            term = ref[...].reshape(2 * observers, members * width)
            total = term if total is None else total + term
        solved = []
        for b in range(members):
            residual = jnp.concatenate([rhs[b][0], rhs[b][1]], axis=0)
            if total is not None:
                residual = residual - total[:, b * width : (b + 1) * width]
            for a in range(b):
                residual = residual - product(solved[a], inside[a][:, :, b * width : (b + 1) * width])
            value = product(residual.reshape(2, observers, width), inverse[b][...])
            solved.append(value.reshape(2, observers, width))
            out[:, :, b * width : (b + 1) * width] = solved[b]

    for k, result in enumerate(results):
        @pl.when(leads(k, members))
        def _(result=result):
            out[...] = result[...]


def held_kernel(group, targets, members, width, *refs):
    out = refs[-1]
    pieces = refs[-1 - members : -1]
    row, col = lax.axis_index("row"), lax.axis_index("col")
    for k, x in zip(targets, refs):
        @pl.when((row == members * group + members - 1) & (col == k))
        def _(x=x):
            total = None
            for t in range(members):
                term = product(x[:, :, t * width : (t + 1) * width], pieces[t][...])
                total = term if total is None else total + term
            out[...] = total.reshape(out.shape)


def merge_kernel(members, sources, *refs):
    outs = refs[-members:]
    width = outs[0].shape[2]
    group, col = lax.div(lax.axis_index("row"), members), lax.axis_index("col")
    for source, places in zip(refs, sources):
        for i, k in places:
            @pl.when((group == i) & (col == k))
            def _(source=source):
                for t in range(members):
                    outs[t][...] = source[:, :, t * width : (t + 1) * width]


def when_kernel(late, members, skip, kernel, *refs):
    inside = lax.axis_index("row") >= members

    @pl.when(inside if late else jnp.logical_not(inside))
    def _():
        kernel(*refs[skip[0] : skip[1]], *refs[skip[2] :])


def prepare_kernel(chunk, chunks, members, who, invert, skip, *refs):
    trail, high, low, room, sems = refs[skip:]
    devices, columns = room.shape[0], room.shape[3]
    wanted = jnp.bool_(False)
    for k in who:
        wanted = wanted | leads(k, members)

    @pl.when(jnp.logical_not(wanted) if invert else wanted)
    def _():
        copies = []
        for i in range(devices):
            start = (i * chunks + chunk) * columns
            copies.append(pltpu.make_async_copy(trail.at[:, :, start : start + columns], room.at[i], sems.at[i]))
            copies[-1].start()
        for i in range(devices):
            copies[i].wait()
            for part in range(2):
                depth = room.shape[2]
                a, b = split(room[i, part])
                high[i, part * depth : (part + 1) * depth] = a
                low[i, part * depth : (part + 1) * depth] = b


def trail_kernel(chunk, chunks, cols, ready, select, odds, members, currents, owner, *refs):
    row = lax.axis_index("row")
    refs = list(refs)
    candidates = [refs.pop(0) for _ in range(members if select else 1)]
    factors = [refs.pop(0) for _ in range(2 if ready else 1)]
    x = refs.pop(0) if select else candidates[0]
    outs = {odd: (refs.pop(0), refs.pop(0)) for odd in odds}
    if select:
        solved, sem = refs
        for t in range(members):
            @pl.when(lax.rem(row, members) == t)
            def _(t=t):
                x[...] = candidates[t][...]
        out = pltpu.make_async_copy(x, solved, sem)
        out.start()
    observers, depth = x.shape[1], x.shape[2]
    if ready:
        high, low = factors
        devices, columns = high.shape[0], high.shape[2]
    else:
        trail, (room, sems) = factors[0], refs
        devices, columns = room.shape[0], room.shape[3]
    half = devices // 2
    work = [(row ^ (2 * e + odd), e, odd) for odd in odds for e in range(half)]
    copies = []
    if not ready:
        for i, (target, _, _) in enumerate(work):
            start = pl.multiple_of((target * chunks + chunk) * columns, LANES)
            copies.append(pltpu.make_async_copy(trail.at[:, :, pl.ds(start, columns)], room.at[i], sems.at[i]))
            copies[-1].start()
    first, second = stacked(x[...])
    if depth % LANES == 0:
        lefts = [split(jnp.concatenate([first, second], axis=1))]
    else:
        lefts = [split(first), split(second)]
    lefts = [(a, jnp.concatenate([a, b], axis=0)) for a, b in lefts]
    share = 2 * depth // len(lefts)
    extra = outs[odds[0]][0].shape[2] - columns
    if extra:
        col = lax.axis_index("col")
        sums = jnp.sum(x[...], axis=1, keepdims=True)
        partial = currents[0:1] * sums[0] - currents[1:2] * sums[1]
        patch = lax.broadcasted_iota(jnp.int32, (observers, depth), 0)
    for i, (target, e, odd) in enumerate(work):
        ref_a, ref_b = outs[odd]
        total = None
        if not ready:
            copies[i].wait()
            whole = room[i].reshape(2 * depth, columns)
        for j, (left, pair) in enumerate(lefts):
            place = slice(j * share, (j + 1) * share)
            if ready:
                right_high, right_low = high[target, place], low[target, place]
            else:
                right_high, right_low = split(whole[place])
            both = dot16(pair, right_high)
            term = both[: 2 * observers] + both[2 * observers :] + dot16(left, right_low)
            total = term if total is None else total + term
        ref_a[e, :, 0:columns] = total[:observers]
        ref_b[e] = total[observers:]
        if extra:
            found = jnp.where(owner[...] == patch + (target * cols + col) * PATCH_DEV, partial, 0.0)
            gradient = jnp.sum(found, axis=1, keepdims=True)
            ref_a[e, :, columns:] = jnp.broadcast_to(gradient, (observers, extra))
    if select:
        out.wait()


def halve(values, axis, bit, rows):
    low = lax.index_in_dim(values, 0, axis, keepdims=False)
    high = lax.index_in_dim(values, 1, axis, keepdims=False)
    arrived = lax.ppermute(high, "row", [(i, i ^ (1 << bit)) for i in range(rows)])
    return low + arrived


def on_device(upper_block, block_inverse, panel_rhs, upper_trail, trail_rhs, currents, owner):
    rows = lax.axis_size("row")
    cols = lax.axis_size("col")
    width = block_inverse.shape[1]
    quarter = upper_block.shape[2]
    observers = panel_rhs.shape[1]
    members = rows // cols
    bits = rows.bit_length() - 1

    def flat(r, c):
        return r * cols + c

    def leader(k):
        return flat(members * k + members - 1, k)

    def send(value, pairs):
        return lax.ppermute(value, ("row", "col"), pairs)

    def near(k):
        return [g for g in ([k - 1, k - 2] if k % 2 and k > 1 else [k - 1]) if g >= 0]

    def far(g):
        return [k for k in range(g + 2, cols) if g not in near(k)]

    pieces = {}

    rounds = {1: [(k, k - 1) for k in range(1, cols, 2)]}
    rounds[2] = [(k, g) for k in range(1, cols) for g in near(k) if (k, g) not in rounds[1]]

    def bring(number):
        for t in range(members):
            moves = rounds[number]
            if moves:
                arrived = send(upper_block, [(flat(members * g + t, k), leader(k)) for k, g in moves])
                for k, g in moves:
                    pieces[k, g, t] = arrived

    bring(1)
    rhs, inverse, inside = [], [], []
    for t in range(members - 1):
        turn = members - 1 - t
        pairs = [(i, i // members * members + (i + turn) % members) for i in range(rows)]
        rhs.append(lax.ppermute(panel_rhs, "row", pairs))
        inverse.append(lax.ppermute(block_inverse, "row", pairs))
        inside.append(lax.ppermute(upper_block, "row", pairs))
    bring(2)
    owner_row = owner.reshape(1, width)
    loaded = [panel_rhs, block_inverse, currents, owner_row, upper_block]
    panel_near, inverse_near, currents_near, owner_near, upper_near = local_call(
        functools.partial(load_kernel, len(loaded)),
        [(a.shape, a.dtype) for a in loaded],
        [],
        loaded,
        [pltpu.SemaphoreType.DMA((len(loaded),))],
        limit=2 << 20,
    )
    rhs.append(panel_near)
    inverse.append(inverse_near)
    upper_rows = [*inside, upper_near]

    columns = upper_trail.shape[2] // rows // CHUNKS
    room = [pltpu.VMEM((rows, 2, width, columns), jnp.float32), pltpu.SemaphoreType.DMA((rows,))]
    part = (2, observers, quarter)
    results, passed, held, early = [], {}, {}, {}
    arrived, sources = [], []

    def spread(value, places):
        arrived.append(send(value, [(leader(g), flat(members * g + members - 1, k)) for g, k in places]))
        sources.append(places)

    ready = []

    def prepare(source, who, invert=False):
        nonlocal ready
        ready = local_call(
            functools.partial(prepare_kernel, 0, CHUNKS, members, who, invert, len(ready)),
            [((rows, 2 * width, columns), jnp.bfloat16)] * 2,
            ready,
            [source],
            room,
            aliases={i: i for i in range(len(ready))},
        )

    for step in range(cols):
        final = step + 1 == cols
        terms = [held[g, step] for g in range(step) if step in far(g)]
        factors = []
        for g in near(step):
            factors += [passed[g, step], *(pieces[step, g, t] for t in range(members))]
        result = local_call(
            functools.partial(step_kernel, step, members, width, len(near(step)), len(terms)),
            [(part, jnp.float32)],
            [*rhs, *inverse, *inside, *terms, *factors, *(results if step == cols - 2 else [])],
        )[0]
        results.append(result)
        if not final:
            passed[step, step + 1] = send(result, [(leader(step), leader(step + 1))])
        if step + 2 < cols and step in near(step + 2):
            passed[step, step + 2] = send(result, [(leader(step), leader(step + 2))])
        for k in far(step):
            early[step, k] = send(result, [(leader(step), flat(members * step + members - 1, k))])
        if far(step):
            term = local_call(
                functools.partial(held_kernel, step, far(step), members, width),
                [(part, jnp.float32)],
                [*(early[step, k] for k in far(step)), *upper_rows],
            )[0]
            for k in far(step):
                held[step, k] = send(term, [(flat(members * step + members - 1, k), leader(k))])
        if step == min(1, cols - 2):
            prepare(after(upper_trail, result), list(range(2, cols)), True)
        if step == cols - 2:
            arrived += [result, *early.values()]
            sources += [[(k, k) for k in range(cols - 1)], *([place] for place in early)]
            for s in range(cols - 1, 0, -1):
                places = [(k, (k + s) % cols) for k in range(cols - 1)]
                spread(result, [place for place in places if place not in early])
            prepare(after(upper_trail, result), list(range(2, cols - 1)))

    arrived += [results[-1]]
    sources += [[(cols - 1, cols - 1)]]
    for s in range(1, cols):
        spread(results[-1], [(cols - 1, (cols - 1 + s) % cols)])
    prepare(after(upper_trail, results[-1]), [k for k in [cols - 1] if k > 1])
    parts = local_call(
        functools.partial(merge_kernel, members, sources),
        [((2, observers, width), jnp.float32)] * members,
        arrived,
        limit=2 << 20,
    )
    candidates = []
    for t in range(members - 1):
        turn = t - (members - 1)
        pairs = [(i, i // members * members + (i + turn) % members) for i in range(rows)]
        candidates.append(lax.ppermute(parts[t], "row", pairs))
    candidates.append(parts[-1])

    half = rows // 2
    out_parts, gradient, factor, solved = [], None, None, None
    small = [currents_near, owner_near]
    for chunk in range(CHUNKS):
        extra = LANES if chunk == 0 else 0
        shapes = [((half, observers, columns + extra), jnp.float32), ((half, observers, columns), jnp.float32)]

        def trail(select, odds, operands, far, scratch):
            return local_call(
                functools.partial(trail_kernel, chunk, CHUNKS, cols, chunk == 0, select, odds, members),
                ([(candidates[0].shape, jnp.float32)] if select else []) + shapes * len(odds),
                [*small, *operands],
                far,
                scratch,
                far_outs=[(candidates[0].shape, jnp.float32)] if select else [],
            )

        if chunk == 0:
            factor, *sent, solved = trail(True, (1,), [*candidates, *ready], [], [pltpu.SemaphoreType.DMA])
            kept = trail(False, (0,), [after(factor, sent[0]), *ready], [], [])
        else:
            kernel = functools.partial(trail_kernel, chunk, CHUNKS, cols, False, False, (1, 0), members)
            outs = shapes * 2
            operands = [*small, factor]
            count = len(operands)
            results = local_call(
                functools.partial(when_kernel, False, members, (0, count, count), kernel),
                outs,
                [*small, after(factor, kept[0])],
                [upper_trail],
                room,
            )
            total = count + len(outs)
            results = local_call(
                functools.partial(when_kernel, True, members, (0, count, total), kernel),
                outs,
                [*operands, *results],
                [upper_trail],
                room,
                aliases={count + i: i for i in range(len(outs))},
            )
            sent, kept = results[:2], results[2:]
        parts = []
        for part in range(2):
            arrived = lax.ppermute(sent[part], "row", [(i, i ^ 1) for i in range(rows)])
            value = kept[part] + arrived
            value = value.reshape((2,) * (bits - 1) + value.shape[1:])
            left = list(range(bits - 1, 0, -1))
            order = left[::-1] if part == 0 else left[:]
            for bit in order:
                value = halve(value, left.index(bit), bit, rows)
                left.remove(bit)
            parts.append(value)
        if extra:
            gradient = parts[0][:PATCH_DEV, columns]
        out_parts.append(jnp.stack([parts[0][:, :columns], parts[1]]))
    updated = trail_rhs - jnp.concatenate(out_parts, axis=2)
    return solved, updated, gradient


def solution(mesh):
    in_specs = (
        P(None, "row", "col"),
        P(None, "row", None),
        P(None, None, "row"),
        P(None, "row", "col"),
        P(None, None, ("col", "row")),
        P(None, "row"),
        P("row"),
    )
    out_specs = (P(None, None, "row"), P(None, None, ("col", "row")), P(("row", "col")))

    return jax.shard_map(on_device, mesh=mesh, in_specs=in_specs, out_specs=out_specs, check_vma=False)
```
